32 devices in a mesh: groups: 2 (over y), text: 4 (over z), image: 4 (over x, core).
Axes of the slice: x: 2, y: 2, z: 4, core: 2. Of those that a mesh axis runs over, the one named last changes fastest.
Arguments:
- text_states: bfloat16 [1024, 8192], P(('groups', 'text')), parts along dimension 0, may hold values from -6 to 6
- grid_levels: bfloat16 [16384, 8192], P(('groups', 'text'), 'image'), parts along dimension 0, may hold values from -8 to 7, as said below
- round_logits: float32 [16384, 8192], P(('groups', 'text'), 'image'), parts along dimension 0, may hold values from -2 to 2
- column_steps: float32 [16384], P(('groups', 'image')), parts along dimension 0, may hold values from 0.0015 to 0.004
- image_keys: bfloat16 [12808, 1024], P('groups', 'image'), parts along dimension 0, may hold values from -500 to 500
- image_values: bfloat16 [12808, 1024], P('groups', 'image'), parts along dimension 0, may hold values from -6 to 6
- target_out: bfloat16 [1024, 8192], P(('groups', 'text'), 'image'), parts along dimension 0, may hold values from -6 to 6
- doc_images: int32 [6], P('groups'), parts along dimension 0, may hold values from 1 to 2, as said below
- image_start: int32 [8], P('groups'), parts along dimension 0, may hold values from 1 to 3, as said below
Outputs:
- rounding_grad: float32 [16384, 8192], P(('groups', 'text'), 'image'), parts along dimension 0
The draws below stay inside these ranges and needn't reach their ends.
There are 2 independent parts, one for each index of `groups`. The reference program is written for one: setup_inputs(seed, part) draws one part's arguments, and reference() takes and returns one part's arrays. A program takes and returns all parts, laid end to end along the dimension named above; each array names one. Nothing has to cross between parts.
Inputs may be any that keep to these rules, and one draw needn't show every extreme that they name: `doc_images`: every document holds one image or more, 4 in all; one document holds exactly 2, and no document more. `image_start`: Nondecreasing; the first image's entry is 1 and the last image's 4 - 1. `grid_levels`: whole numbers.
All inputs are finite; a program needn't handle non-finite values.
Results may differ from the reference program's by a relative error of at most 0.015.
Values may be sent and summed in bfloat16 or wider, within the bound.
A program may use at most 256 MiB of HBM per device.

```python
import math
import jax
import jax.numpy as jnp
from jax import lax

D = 8192
H = 64
KVH = 8
HD = 128
IMAGES = 4
IMG_TOK = 1601
SPAN = 128
DOCS = 3
TOKENS = 512
SPANS = 4


def draw_grid_levels(key, part):
    return jax.random.randint(key, (D, D), -8, 8).astype(jnp.float32).astype(jnp.bfloat16)


def draw_image_keys(key, part):
    rows = IMAGES * IMG_TOK
    first_key = jax.random.fold_in(key, 0)
    base = jax.random.normal(first_key, (rows, KVH * HD), jnp.float32)
    return base.astype(jnp.bfloat16)


def draw_doc_images(key, part):
    heavy_key, cut_key = jax.random.split(jax.random.fold_in(key, 7))
    heavy_count = IMAGES // 2
    rest = IMAGES - heavy_count
    others = DOCS - 1
    heavy = jax.random.randint(heavy_key, (), 0, DOCS)
    order = jax.random.permutation(cut_key, rest - 1) + 1
    cuts = jnp.sort(order[:others - 1]).astype(jnp.int32)
    edges = jnp.concatenate([jnp.zeros((1,), jnp.int32), cuts, jnp.full((1,), rest, jnp.int32)])
    pieces = (edges[1:] - edges[:-1]).astype(jnp.int32)
    positions = jnp.arange(DOCS, dtype=jnp.int32)
    slot = positions - (positions > heavy).astype(jnp.int32)
    slot = jnp.clip(slot, 0, others - 1)
    picked = jnp.sum(jnp.where(jnp.arange(others, dtype=jnp.int32)[None, :] == slot[:, None], pieces[None, :], 0), axis=1)
    return jnp.where(positions == heavy, heavy_count, picked).astype(jnp.int32)


def draw_image_start(key, part):
    drawn = jax.random.randint(key, (IMAGES,), 1, SPANS - 1)
    ordered = jnp.sort(drawn)
    ordered = ordered.at[0].set(1)
    return ordered.at[IMAGES - 1].set(SPANS - 1).astype(jnp.int32)


def steps_of(key, extent, cuts, low, largest):
    def one(dim, blocks):
        steps = jax.random.uniform(jax.random.fold_in(jax.random.fold_in(key, 6), dim), (blocks,), jnp.float32, low / len(cuts), largest / len(cuts))
        return jnp.repeat(jnp.exp(steps), extent[dim] // blocks).reshape((-1,) + (1,) * (len(extent) - dim - 1))

    gain = one(*cuts[0])
    for cut in cuts[1:]:
        gain = gain * one(*cut)
    return gain


def scatter_about(stream_key, shape, spread, limit, cuts=(), held_as=jnp.bfloat16):
    entries = jax.random.normal(stream_key, shape, jnp.float32) * spread
    if len(cuts) > 0:
        entries = steps_of(stream_key, shape, cuts, -0.22, 0.18) * entries
    return jnp.clip(entries, min=-limit, max=limit).astype(held_as)


def setup_inputs(seed: int = 0, part: int = 0) -> dict:
    key_of = jax.random.split(jax.random.key(seed), 10)
    own_keys = jax.random.split(jax.random.fold_in(key_of[9], part), 10)
    text_states = scatter_about(own_keys[0], (TOKENS, D), 1.0, 6.0, ((0, 4),))
    grid_levels = draw_grid_levels(jax.random.fold_in(jax.random.fold_in(key_of[9], part), 71), part)
    round_logits = jnp.clip(jax.random.uniform(own_keys[2], (D, D), jnp.float32, -2.0, 2.0) * steps_of(own_keys[2], (D, D), ((0, 4), (1, 4)), -0.4, 0.0), -2.0, 2.0)
    column_steps = jnp.clip(jnp.exp(math.log(0.004) - 0.9808293 * jax.random.uniform(own_keys[3], (D,), jnp.float32) ** steps_of(own_keys[3], (D,), ((0, 4),), -0.2, 0.2)), 0.0015, 0.004)
    image_keys = draw_image_keys(jax.random.fold_in(jax.random.fold_in(key_of[9], part), 71), part)
    image_values = scatter_about(own_keys[5], (IMAGES * IMG_TOK, KVH * HD), 1.0, 6.0, ((1, 4),))
    target_out = scatter_about(own_keys[6], (TOKENS, D), 1.0, 6.0, ((0, 4), (1, 4)))
    doc_images = draw_doc_images(jax.random.fold_in(jax.random.fold_in(key_of[9], part), 71), part)
    image_start = draw_image_start(jax.random.fold_in(jax.random.fold_in(key_of[9], part), 71), part)
    return {"text_states": text_states, "grid_levels": grid_levels, "round_logits": round_logits, "column_steps": column_steps, "image_keys": image_keys, "image_values": image_values, "target_out": target_out, "doc_images": doc_images, "image_start": image_start}


def visibility(span_ids, doc_images, image_start, total_spans):
    images = image_start.shape[0]
    documents = doc_images.shape[0]
    doc_ends = jnp.cumsum(doc_images).astype(jnp.int32)
    positions = jnp.arange(images, dtype=jnp.int32)
    doc_of = lax.optimization_barrier(jnp.sum((positions[:, None] >= doc_ends[None, :]).astype(jnp.int32), axis=1))
    doc_index = jnp.arange(documents, dtype=jnp.int32)
    end_of = lax.optimization_barrier(jnp.sum(jnp.where(doc_index[None, :] == doc_of[:, None], doc_ends[None, :], 0), axis=1))
    stop_at = lax.optimization_barrier(jnp.sum(jnp.where(positions[None, :] == end_of[:, None], image_start[None, :], 0), axis=1))
    stop_at = stop_at + jnp.where(end_of >= images, total_spans, 0)
    return (span_ids[:, None] >= image_start[None, :]) & (span_ids[:, None] < stop_at[None, :])

def head_grad(queries, keys, values, target, visible):
    tokens_here = queries.shape[0]
    kv_heads = queries.shape[1]
    per_group = queries.shape[2]
    head_size = queries.shape[3]
    scaling = head_size ** (-0.5)
    query_wide = queries.astype(jnp.float32)
    shape = (kv_heads, per_group, tokens_here)

    def tile_of(which):
        keys_now = lax.dynamic_slice_in_dim(keys, which * IMG_TOK, IMG_TOK, 0).astype(jnp.float32)
        values_now = lax.dynamic_slice_in_dim(values, which * IMG_TOK, IMG_TOK, 0).astype(jnp.float32)
        scores = jnp.einsum('tkgd,nkd->kgtn', query_wide, keys_now) * scaling
        seen = lax.dynamic_index_in_dim(visible, which, 1, keepdims=False)
        return (scores, keys_now, values_now, seen[None, None, :])

    def forward(which, state):
        running, total, accum = state
        scores, keys_now, values_now, seen = tile_of(which)
        peak = jnp.where(seen, jnp.maximum(running, lax.optimization_barrier(jnp.max(scores, axis=-1))), running)
        weights = jnp.where(seen[..., None], jnp.exp(scores - peak[..., None]), 0.0)
        fade = jnp.exp(running - peak)
        total = total * fade + lax.optimization_barrier(jnp.sum(weights, axis=-1))
        rounded = lax.optimization_barrier(weights.astype(jnp.bfloat16)).astype(jnp.float32)
        accum = accum * fade[..., None] + jnp.einsum('kgtn,nkd->kgtd', rounded, values_now)
        return (peak, total, accum)
    start_state = (jnp.full(shape, -1e+30, jnp.float32), jnp.zeros(shape, jnp.float32), jnp.zeros(shape + (head_size,), jnp.float32))
    running, total, accum = lax.fori_loop(0, IMAGES, forward, start_state)
    denom = jnp.maximum(total, 1.0)
    attended = accum / denom[..., None]
    out_grad = (1024.0 * (attended - target)).astype(jnp.bfloat16)
    out_wide = out_grad.astype(jnp.float32)
    delta = lax.optimization_barrier(jnp.sum(out_wide * attended, axis=-1))

    def backward(which, grad_acc):
        scores, keys_now, values_now, seen = tile_of(which)
        probs = jnp.where(seen[..., None], jnp.exp(scores - running[..., None]), 0.0) / denom[..., None]
        dprob = jnp.einsum('kgtd,nkd->kgtn', out_wide, values_now)
        score_grad = (probs * (dprob - delta[..., None]) * scaling).astype(jnp.bfloat16)
        score_wide = lax.optimization_barrier(score_grad).astype(jnp.float32)
        return grad_acc + jnp.einsum('kgtn,nkd->kgtd', score_wide, keys_now)
    grad_sum = lax.fori_loop(0, IMAGES, backward, jnp.zeros(shape + (head_size,), jnp.float32))
    return grad_sum.astype(jnp.bfloat16)

def reference(text_states, grid_levels, round_logits, column_steps, image_keys, image_values, target_out, doc_images, image_start):
    per_group = H // KVH
    sigmoid_v = jax.nn.sigmoid(round_logits)
    soft = 1.2 * sigmoid_v - 0.1
    weight_q = (column_steps[None, :] * (grid_levels.astype(jnp.float32) + soft)).astype(jnp.bfloat16)
    queries = jnp.dot(text_states, weight_q, preferred_element_type=jnp.float32).astype(jnp.bfloat16)
    span_ids = jnp.arange(TOKENS, dtype=jnp.int32) // SPAN
    visible = visibility(span_ids, doc_images, image_start, SPANS)
    query_heads = queries.reshape(TOKENS, KVH, 1, per_group, HD).transpose(1, 0, 2, 3, 4)
    key_heads = image_keys.reshape(IMAGES * IMG_TOK, KVH, 1, HD).transpose(1, 0, 2, 3)
    value_heads = image_values.reshape(IMAGES * IMG_TOK, KVH, 1, HD).transpose(1, 0, 2, 3)
    target_heads = target_out.astype(jnp.float32).reshape(TOKENS, KVH, 1, per_group, HD).transpose(1, 2, 3, 0, 4)

    def one_head(bundle):
        return head_grad(bundle[0], bundle[1], bundle[2], bundle[3], visible)
    grads = lax.map(one_head, (query_heads, key_heads, value_heads, target_heads))
    query_grad = grads.transpose(3, 0, 1, 2, 4).reshape(TOKENS, D)
    weight_grad = jnp.dot(text_states.T, query_grad, preferred_element_type=jnp.float32)
    hprime = 1.2 * sigmoid_v * (1.0 - sigmoid_v)
    centered = 2.0 * soft - 1.0
    return (weight_grad * column_steps[None, :] - 4.0 * centered * centered * centered) * hprime
```

```python
import jax
import jax.numpy as jnp
from jax import lax
from jax.sharding import PartitionSpec as P

H = 64
KVH = 8
HD = 128
IMAGES = 4
IMG_TOK = 1601
SPAN = 128


def visibility(span_ids, doc_images, image_start, total_spans):
    images = image_start.shape[0]
    documents = doc_images.shape[0]
    doc_ends = jnp.cumsum(doc_images)
    positions = jnp.arange(images, dtype=jnp.int32)
    doc_of = jnp.sum((positions[:, None] >= doc_ends[None, :]).astype(jnp.int32), axis=1)
    doc_index = jnp.arange(documents, dtype=jnp.int32)
    end_of = jnp.sum(jnp.where(doc_index[None, :] == doc_of[:, None], doc_ends[None, :], 0), axis=1)
    stop_at = jnp.sum(
        jnp.where(positions[None, :] == end_of[:, None], image_start[None, :], 0), axis=1
    )
    stop_at = stop_at + jnp.where(end_of >= images, total_spans, 0)
    return (span_ids[:, None] >= image_start[None, :]) & (span_ids[:, None] < stop_at[None, :])


def head_grad(queries, keys, values, target, visible):
    tokens_here = queries.shape[0]
    kv_heads = queries.shape[1]
    per_group = queries.shape[2]
    head_size = queries.shape[3]
    scaling = head_size ** (-0.5)
    shape = (kv_heads, per_group, tokens_here)

    def tile_of(which):
        keys_now = lax.dynamic_slice_in_dim(keys, which * IMG_TOK, IMG_TOK, 0)
        values_now = lax.dynamic_slice_in_dim(values, which * IMG_TOK, IMG_TOK, 0)
        scores = (
            jnp.einsum("tkgd,nkd->kgtn", queries, keys_now, preferred_element_type=jnp.float32)
            * scaling
        )
        return (scores, keys_now, values_now)

    def seen_of(which):
        return lax.dynamic_index_in_dim(visible, which, 1, keepdims=False)

    def forward(which, state):
        seen_rows = seen_of(which)
        running, total, accum = state
        scores, keys_now, values_now = tile_of(which)
        seen = seen_rows[None, None, :]
        peak = jnp.where(seen, jnp.maximum(running, jnp.max(scores, axis=-1)), running)
        weights = jnp.where(seen[..., None], jnp.exp(scores - peak[..., None]), 0.0)
        fade = jnp.exp(running - peak)
        total = total * fade + jnp.sum(weights, axis=-1)
        product = jnp.einsum(
            "kgtn,nkd->kgtd",
            weights.astype(jnp.bfloat16),
            values_now,
            preferred_element_type=jnp.float32,
        )
        return (peak, total, accum * fade[..., None] + product)

    start_state = (
        jnp.full(shape, -1e30, jnp.float32),
        jnp.zeros(shape, jnp.float32),
        jnp.zeros(shape + (head_size,), jnp.float32),
    )
    running, total, accum = lax.fori_loop(0, IMAGES, forward, start_state)
    denom = jnp.maximum(total, 1.0)
    attended = accum / denom[..., None]
    out_grad = (1024.0 * (attended - target)).astype(jnp.bfloat16)
    delta = jnp.sum(out_grad.astype(jnp.float32) * attended, axis=-1)

    def backward(which, grad_acc):
        seen_rows = seen_of(which)
        scores, keys_now, values_now = tile_of(which)
        seen = seen_rows[None, None, :]
        probs = (
            jnp.where(seen[..., None], jnp.exp(scores - running[..., None]), 0.0) / denom[..., None]
        )
        dprob = jnp.einsum(
            "kgtd,nkd->kgtn", out_grad, values_now, preferred_element_type=jnp.float32
        )
        score_grad = (probs * (dprob - delta[..., None]) * scaling).astype(jnp.bfloat16)
        return grad_acc + jnp.einsum(
            "kgtn,nkd->kgtd", score_grad, keys_now, preferred_element_type=jnp.float32
        )

    grad_sum = lax.fori_loop(0, IMAGES, backward, jnp.zeros(shape + (head_size,), jnp.float32))
    return grad_sum.astype(jnp.bfloat16)


def per_device(
    text_states,
    grid_levels,
    round_logits,
    column_steps,
    image_keys,
    image_values,
    target_out,
    doc_images,
    image_start,
):
    tok_dev = text_states.shape[0]
    out_cols = grid_levels.shape[1]
    n_text = lax.axis_size("text")
    per_group = H // KVH
    kvh_dev = image_keys.shape[1] // HD
    sigmoid_v = jax.nn.sigmoid(round_logits)
    soft = 1.2 * sigmoid_v - 0.1
    weight_q = (column_steps[None, :] * (grid_levels.astype(jnp.float32) + soft)).astype(
        jnp.bfloat16
    )
    spread = lax.all_to_all(text_states, "text", split_axis=1, concat_axis=0, tiled=True)
    q_part = jnp.dot(spread, weight_q, preferred_element_type=jnp.float32)
    q_sum = lax.psum_scatter(q_part, "text", scatter_dimension=0, tiled=True)
    queries = q_sum.astype(jnp.bfloat16)
    first_token = lax.axis_index("text") * tok_dev
    span_ids = (first_token + jnp.arange(tok_dev, dtype=jnp.int32)) // SPAN
    visible = visibility(span_ids, doc_images, image_start, n_text * tok_dev // SPAN)
    query_tiles = queries.reshape(tok_dev, kvh_dev, per_group, HD)
    key_tiles = image_keys.reshape(image_keys.shape[0], kvh_dev, HD)
    value_tiles = image_values.reshape(image_values.shape[0], kvh_dev, HD)
    target_tiles = (
        target_out.astype(jnp.float32)
        .reshape(tok_dev, kvh_dev, per_group, HD)
        .transpose(1, 2, 0, 3)
    )
    grads = head_grad(query_tiles, key_tiles, value_tiles, target_tiles, visible)
    query_grad = grads.transpose(2, 0, 1, 3).reshape(tok_dev, out_cols)
    weight_grad = lax.dot_general(
        spread,
        lax.all_gather(query_grad, "text", axis=0, tiled=True),
        (((0,), (0,)), ((), ())),
        preferred_element_type=jnp.float32,
    )
    hprime = 1.2 * sigmoid_v * (1.0 - sigmoid_v)
    centered = 2.0 * soft - 1.0
    return (weight_grad * column_steps[None, :] - 4.0 * centered * centered * centered) * hprime


def solution(mesh):
    placed = (
        P(("groups", "text"), None),
        P(("groups", "text"), "image"),
        P(("groups", "text"), "image"),
        P(("groups", "image")),
        P("groups", "image"),
        P("groups", "image"),
        P(("groups", "text"), "image"),
        P("groups"),
        P("groups"),
    )
    return jax.shard_map(
        per_device,
        mesh=mesh,
        in_specs=placed,
        out_specs=P(("groups", "text"), "image"),
        check_vma=False,
    )
```

```python
import functools

import jax
import jax.numpy as jnp
from jax import lax
from jax.experimental import pallas as pl
from jax.experimental.pallas import tpu as pltpu
from jax.sharding import PartitionSpec as P

H = 64
KVH = 8
HD = 128
IMG_TOK = 1601
SPAN = 128
MAX_SEEN = 2
KEYS = MAX_SEEN * IMG_TOK
KEYS_PAD = -(-KEYS // 256) * 256
CHUNKS = 2
NEG = -1e30


def visibility(span_ids, doc_images, image_start, total_spans):
    images = image_start.shape[0]
    documents = doc_images.shape[0]
    doc_ends = jnp.cumsum(doc_images)
    positions = jnp.arange(images, dtype=jnp.int32)
    doc_of = jnp.sum((positions[:, None] >= doc_ends[None, :]).astype(jnp.int32), axis=1)
    doc_index = jnp.arange(documents, dtype=jnp.int32)
    end_of = jnp.sum(jnp.where(doc_index[None, :] == doc_of[:, None], doc_ends[None, :], 0), axis=1)
    stop_at = jnp.sum(
        jnp.where(positions[None, :] == end_of[:, None], image_start[None, :], 0), axis=1
    )
    stop_at = stop_at + jnp.where(end_of >= images, total_spans, 0)
    return (span_ids[:, None] >= image_start[None, :]) & (span_ids[:, None] < stop_at[None, :])


NT = (((1,), (1,)), ((), ()))


def attention_kernel(bounds_ref, q_ref, k_ref, v_ref, t_ref, o_ref):
    first = bounds_ref[0]
    stop = bounds_ref[1]
    scaling = HD ** (-0.5)
    tokens, width = q_ref.shape
    heads = width // HD

    def stacked(ref):
        return jnp.concatenate([ref[:, h * HD : (h + 1) * HD] for h in range(heads)], axis=0)

    @pl.when(stop <= first)
    def _():
        o_ref[...] = jnp.zeros_like(o_ref)

    @pl.when(stop > first)
    def _():
        row = lax.broadcasted_iota(jnp.int32, (1, KEYS_PAD), 1)
        bias = jnp.where((row >= first) & (row < stop), 0.0, NEG)
        q = stacked(q_ref).astype(jnp.bfloat16)
        k = k_ref[...]
        v = v_ref[...]
        s = lax.dot_general(q, k, NT, preferred_element_type=jnp.float32) * scaling + bias
        peak = jnp.max(s, axis=-1, keepdims=True)
        w = jnp.exp(s - peak)
        total = jnp.sum(w, axis=-1, keepdims=True)
        acc = jnp.dot(w.astype(jnp.bfloat16), v, preferred_element_type=jnp.float32)
        inv = 1.0 / jnp.maximum(total, 1.0)
        attended = acc * inv
        out_grad = (1024.0 * (attended - stacked(t_ref).astype(jnp.float32))).astype(jnp.bfloat16)
        delta = jnp.sum(out_grad.astype(jnp.float32) * attended, axis=-1, keepdims=True)
        dp = lax.dot_general(out_grad, v, NT, preferred_element_type=jnp.float32)
        ds = (w * ((dp - delta) * (inv * scaling))).astype(jnp.bfloat16)
        g = jnp.dot(ds, k, preferred_element_type=jnp.float32).astype(o_ref.dtype)
        for h in range(heads):
            o_ref[:, h * HD : (h + 1) * HD] = g[h * tokens : (h + 1) * tokens]


def attention(bounds, queries, keys, values, target, chunk):
    tokens, width = queries.shape
    pair = 2 * HD
    steps = width // pair
    group = (H // KVH) * HD
    base = chunk * steps

    def kv_map(i, b):
        return (0, ((base + i) * pair) // group)

    return pl.pallas_call(
        attention_kernel,
        out_shape=jax.ShapeDtypeStruct((tokens, width), jnp.bfloat16),
        grid_spec=pltpu.PrefetchScalarGridSpec(
            num_scalar_prefetch=1,
            grid=(steps,),
            in_specs=[
                pl.BlockSpec((tokens, pair), lambda i, b: (0, i)),
                pl.BlockSpec((KEYS_PAD, HD), kv_map),
                pl.BlockSpec((KEYS_PAD, HD), kv_map),
                pl.BlockSpec((tokens, pair), lambda i, b: (0, base + i)),
            ],
            out_specs=pl.BlockSpec((tokens, pair), lambda i, b: (0, i)),
        ),
        compiler_params=pltpu.CompilerParams(vmem_limit_bytes=44 << 20),
        cost_estimate=pl.CostEstimate(
            flops=20 * tokens * width * KEYS_PAD // 2,
            bytes_accessed=4 * KEYS_PAD * HD + 8 * tokens * width,
            transcendentals=tokens * (width // HD) * KEYS_PAD,
        ),
        name="attention",
    )(bounds, queries, keys, values, target)


def final_kernel(x_ref, g_ref, r_ref, c_ref, *rest):
    o_ref = rest[-1]
    wg = jnp.dot(x_ref[...], g_ref[...], preferred_element_type=jnp.float32)
    t = jnp.tanh(0.5 * r_ref[...])
    t2 = t * t
    o_ref[...] = (wg * (0.3 * c_ref[...]) - (4.0 * 1.728 * 0.3) * (t2 * t)) * (1.0 - t2)


def final(spread_t, grad, logits, steps, previous, chunk):
    rows, tokens = spread_t.shape
    width = grad.shape[1]
    tm = 256
    in_specs = [
        pl.BlockSpec((tm, tokens), lambda i: (i, 0)),
        pl.BlockSpec((tokens, width), lambda i: (0, 0)),
        pl.BlockSpec((tm, width), lambda i: (i, chunk)),
        pl.BlockSpec((1, width), lambda i: (0, chunk)),
    ]
    args = [spread_t, grad, logits, steps]
    aliases = {}
    if previous is not None:
        in_specs.append(pl.BlockSpec(memory_space=pl.ANY))
        args.append(previous)
        aliases = {4: 0}
    return pl.pallas_call(
        final_kernel,
        out_shape=jax.ShapeDtypeStruct(logits.shape, jnp.float32),
        grid=(rows // tm,),
        in_specs=in_specs,
        out_specs=pl.BlockSpec((tm, width), lambda i: (i, chunk)),
        input_output_aliases=aliases,
        compiler_params=pltpu.CompilerParams(vmem_limit_bytes=40 << 20),
        cost_estimate=pl.CostEstimate(
            flops=2 * rows * tokens * width,
            bytes_accessed=8 * rows * width + 2 * tokens * (rows + width),
            transcendentals=rows * width,
        ),
        name="final",
    )(*args)


def per_device(
    text_states,
    grid_levels,
    round_logits,
    column_steps,
    image_keys,
    image_values,
    target_out,
    doc_images,
    image_start,
):
    tok_dev = text_states.shape[0]
    out_cols = grid_levels.shape[1]
    n_text = lax.axis_size("text")
    assert tok_dev == SPAN
    images = image_start.shape[0]
    steps_row = column_steps[None, :]

    spread = lax.all_to_all(text_states, "text", split_axis=1, concat_axis=0, tiled=True)
    soft = 0.5 + 0.6 * jnp.tanh(0.5 * round_logits)
    weight_q = (steps_row * (grid_levels.astype(jnp.float32) + soft)).astype(jnp.bfloat16)
    weight_q = lax.optimization_barrier(weight_q)

    span_ids = jnp.reshape(lax.axis_index("text"), (1,)).astype(jnp.int32)
    visible = visibility(span_ids, doc_images, image_start, n_text)[0]
    seen_before = jnp.cumsum(visible.astype(jnp.int32))
    count = seen_before[-1]
    lowest = jnp.sum((seen_before == 0).astype(jnp.int32))
    base = jnp.minimum(lowest, images - MAX_SEEN)
    first = (lowest - base) * IMG_TOK
    bounds = jnp.stack([first, first + count * IMG_TOK]).astype(jnp.int32)

    def window(array):
        rows = lax.dynamic_slice_in_dim(array, base * IMG_TOK, KEYS, 0)
        return jnp.pad(rows, ((0, KEYS_PAD - KEYS), (0, 0)))

    keys = window(image_keys)
    values = window(image_values)

    width = out_cols // CHUNKS
    grads = []
    sums = []
    for c in range(CHUNKS):
        part = jnp.dot(
            spread, weight_q[:, c * width : (c + 1) * width], preferred_element_type=jnp.float32
        )
        sums.append(lax.psum_scatter(part, "text", scatter_dimension=0, tiled=True))
    for c in range(CHUNKS):
        local = attention(bounds, sums[c], keys, values, target_out, c)
        grads.append(lax.all_gather(local, "text", axis=0, tiled=True))
    spread_t = spread.T
    result = None
    for c in range(CHUNKS):
        result = final(spread_t, grads[c], round_logits, steps_row, result, c)
    return result


def solution(mesh):
    placed = (
        P(("groups", "text"), None),
        P(("groups", "text"), "image"),
        P(("groups", "text"), "image"),
        P(("groups", "image")),
        P("groups", "image"),
        P("groups", "image"),
        P(("groups", "text"), "image"),
        P("groups"),
        P("groups"),
    )
    return jax.shard_map(
        per_device,
        mesh=mesh,
        in_specs=placed,
        out_specs=P(("groups", "text"), "image"),
        check_vma=False,
    )
```

```python
import functools

import jax
import jax.numpy as jnp
from jax import lax
from jax.experimental import pallas as pl
from jax.experimental.pallas import tpu as pltpu
from jax.sharding import PartitionSpec as P

H = 64
KVH = 8
HD = 128
IMG_TOK = 1601
SPAN = 128
MAX_SEEN = 2
KEYS = MAX_SEEN * IMG_TOK
KEYS_PAD = -(-KEYS // 256) * 256
CHUNKS = 2
NEG = -1e30


def visibility(span_ids, doc_images, image_start, total_spans):
    images = image_start.shape[0]
    documents = doc_images.shape[0]
    doc_ends = jnp.cumsum(doc_images)
    positions = jnp.arange(images, dtype=jnp.int32)
    doc_of = jnp.sum((positions[:, None] >= doc_ends[None, :]).astype(jnp.int32), axis=1)
    doc_index = jnp.arange(documents, dtype=jnp.int32)
    end_of = jnp.sum(jnp.where(doc_index[None, :] == doc_of[:, None], doc_ends[None, :], 0), axis=1)
    stop_at = jnp.sum(
        jnp.where(positions[None, :] == end_of[:, None], image_start[None, :], 0), axis=1
    )
    stop_at = stop_at + jnp.where(end_of >= images, total_spans, 0)
    return (span_ids[:, None] >= image_start[None, :]) & (span_ids[:, None] < stop_at[None, :])


NT = (((1,), (1,)), ((), ()))


def attention_kernel(bounds_ref, q_ref, k_ref, v_ref, t_ref, o_ref):
    first = bounds_ref[0]
    stop = bounds_ref[1]
    scaling = HD ** (-0.5)
    tokens, width = q_ref.shape
    heads = width // HD

    def stacked(ref):
        return jnp.concatenate([ref[:, h * HD : (h + 1) * HD] for h in range(heads)], axis=0)

    @pl.when(stop <= first)
    def _():
        o_ref[...] = jnp.zeros_like(o_ref)

    @pl.when(stop > first)
    def _():
        row = lax.broadcasted_iota(jnp.int32, (1, KEYS_PAD), 1)
        bias = jnp.where((row >= first) & (row < stop), 0.0, NEG)
        q = stacked(q_ref).astype(jnp.bfloat16)
        k = k_ref[...]
        v = v_ref[...]
        s = lax.dot_general(q, k, NT, preferred_element_type=jnp.float32) * scaling + bias
        peak = jnp.max(s, axis=-1, keepdims=True)
        w = jnp.exp(s - peak)
        total = jnp.sum(w, axis=-1, keepdims=True)
        acc = jnp.dot(w.astype(jnp.bfloat16), v, preferred_element_type=jnp.float32)
        inv = 1.0 / jnp.maximum(total, 1.0)
        attended = acc * inv
        out_grad = (1024.0 * (attended - stacked(t_ref).astype(jnp.float32))).astype(jnp.bfloat16)
        delta = jnp.sum(out_grad.astype(jnp.float32) * attended, axis=-1, keepdims=True)
        dp = lax.dot_general(out_grad, v, NT, preferred_element_type=jnp.float32)
        ds = (w * ((dp - delta) * (inv * scaling))).astype(jnp.bfloat16)
        g = jnp.dot(ds, k, preferred_element_type=jnp.float32).astype(o_ref.dtype)
        for h in range(heads):
            o_ref[:, h * HD : (h + 1) * HD] = g[h * tokens : (h + 1) * tokens]


def attention(bounds, queries, keys, values, target, chunk):
    tokens, width = queries.shape
    pair = 2 * HD
    steps = width // pair
    group = (H // KVH) * HD
    base = chunk * steps

    def kv_map(i, b):
        return (0, ((base + i) * pair) // group)

    return pl.pallas_call(
        attention_kernel,
        out_shape=jax.ShapeDtypeStruct((tokens, width), jnp.bfloat16),
        grid_spec=pltpu.PrefetchScalarGridSpec(
            num_scalar_prefetch=1,
            grid=(steps,),
            in_specs=[
                pl.BlockSpec((tokens, pair), lambda i, b: (0, i)),
                pl.BlockSpec((KEYS_PAD, HD), kv_map),
                pl.BlockSpec((KEYS_PAD, HD), kv_map),
                pl.BlockSpec((tokens, pair), lambda i, b: (0, base + i)),
            ],
            out_specs=pl.BlockSpec((tokens, pair), lambda i, b: (0, i)),
        ),
        compiler_params=pltpu.CompilerParams(vmem_limit_bytes=44 << 20),
        cost_estimate=pl.CostEstimate(
            flops=20 * tokens * width * KEYS_PAD // 2,
            bytes_accessed=4 * KEYS_PAD * HD + 8 * tokens * width,
            transcendentals=tokens * (width // HD) * KEYS_PAD,
        ),
        name="attention",
    )(bounds, queries, keys, values, target)


def final_kernel(x_ref, g_ref, r_ref, c_ref, *rest):
    o_ref = rest[-1]
    wg = jnp.dot(x_ref[...], g_ref[...], preferred_element_type=jnp.float32)
    t = jnp.tanh(0.5 * r_ref[...])
    t2 = t * t
    o_ref[...] = (wg * (0.3 * c_ref[...]) - (4.0 * 1.728 * 0.3) * (t2 * t)) * (1.0 - t2)


def final(spread_t, grad, logits, steps, previous, chunk):
    rows, tokens = spread_t.shape
    width = grad.shape[1]
    tm = 256
    in_specs = [
        pl.BlockSpec((tm, tokens), lambda i: (i, 0)),
        pl.BlockSpec((tokens, width), lambda i: (0, 0)),
        pl.BlockSpec((tm, width), lambda i: (i, chunk)),
        pl.BlockSpec((1, width), lambda i: (0, chunk)),
    ]
    args = [spread_t, grad, logits, steps]
    aliases = {}
    if previous is not None:
        in_specs.append(pl.BlockSpec(memory_space=pl.ANY))
        args.append(previous)
        aliases = {4: 0}
    return pl.pallas_call(
        final_kernel,
        out_shape=jax.ShapeDtypeStruct(logits.shape, jnp.float32),
        grid=(rows // tm,),
        in_specs=in_specs,
        out_specs=pl.BlockSpec((tm, width), lambda i: (i, chunk)),
        input_output_aliases=aliases,
        compiler_params=pltpu.CompilerParams(vmem_limit_bytes=40 << 20),
        cost_estimate=pl.CostEstimate(
            flops=2 * rows * tokens * width,
            bytes_accessed=8 * rows * width + 2 * tokens * (rows + width),
            transcendentals=rows * width,
        ),
        name="final",
    )(*args)


def per_device(
    text_states,
    grid_levels,
    round_logits,
    column_steps,
    image_keys,
    image_values,
    target_out,
    doc_images,
    image_start,
):
    tok_dev = text_states.shape[0]
    out_cols = grid_levels.shape[1]
    n_text = lax.axis_size("text")
    assert tok_dev == SPAN
    images = image_start.shape[0]
    steps_row = column_steps[None, :]

    n_image = lax.axis_size("image")
    share = text_states.shape[1] // (n_text * n_image)
    own = lax.dynamic_index_in_dim(
        text_states.reshape(tok_dev, n_text, n_image, share),
        lax.axis_index("image"),
        2,
        keepdims=False,
    )
    own = lax.all_to_all(own.transpose(1, 0, 2), "text", split_axis=0, concat_axis=0, tiled=True)
    shares = lax.all_gather(own.reshape(n_text * tok_dev, share), "image", axis=0)
    spread = shares.transpose(1, 0, 2).reshape(n_text * tok_dev, n_image * share)
    soft = 0.5 + 0.6 * jnp.tanh(0.5 * round_logits)
    weight_q = (steps_row * (grid_levels.astype(jnp.float32) + soft)).astype(jnp.bfloat16)
    weight_q = lax.optimization_barrier(weight_q)

    span_ids = jnp.reshape(lax.axis_index("text"), (1,)).astype(jnp.int32)
    visible = visibility(span_ids, doc_images, image_start, n_text)[0]
    seen_before = jnp.cumsum(visible.astype(jnp.int32))
    count = seen_before[-1]
    lowest = jnp.sum((seen_before == 0).astype(jnp.int32))
    base = jnp.minimum(lowest, images - MAX_SEEN)
    first = (lowest - base) * IMG_TOK
    bounds = jnp.stack([first, first + count * IMG_TOK]).astype(jnp.int32)

    def window(array):
        rows = lax.dynamic_slice_in_dim(array, base * IMG_TOK, KEYS, 0)
        return jnp.pad(rows, ((0, KEYS_PAD - KEYS), (0, 0)))

    keys = window(image_keys)
    values = window(image_values)

    width = out_cols // CHUNKS
    grads = []
    sums = []
    for c in range(CHUNKS):
        part = jnp.dot(
            spread, weight_q[:, c * width : (c + 1) * width], preferred_element_type=jnp.float32
        )
        sums.append(lax.psum_scatter(part, "text", scatter_dimension=0, tiled=True))
    for c in range(CHUNKS):
        local = attention(bounds, sums[c], keys, values, target_out, c)
        grads.append(lax.all_gather(local, "text", axis=0, tiled=True))
    spread_t = spread.T
    result = None
    for c in range(CHUNKS):
        result = final(spread_t, grads[c], round_logits, steps_row, result, c)
    return result


def solution(mesh):
    placed = (
        P(("groups", "text"), None),
        P(("groups", "text"), "image"),
        P(("groups", "text"), "image"),
        P(("groups", "image")),
        P("groups", "image"),
        P("groups", "image"),
        P(("groups", "text"), "image"),
        P("groups"),
        P("groups"),
    )
    return jax.shard_map(
        per_device,
        mesh=mesh,
        in_specs=placed,
        out_specs=P(("groups", "text"), "image"),
        check_vma=False,
    )
```

```python
import functools

import jax
import jax.numpy as jnp
from jax import lax
from jax.experimental import pallas as pl
from jax.experimental.pallas import tpu as pltpu
from jax.sharding import PartitionSpec as P

H = 64
KVH = 8
HD = 128
IMG_TOK = 1601
SPAN = 128
MAX_SEEN = 2
KEYS = MAX_SEEN * IMG_TOK
KEYS_PAD = -(-KEYS // 256) * 256
CHUNKS = 2
NEG = -1e30


def visibility(span_ids, doc_images, image_start, total_spans):
    images = image_start.shape[0]
    documents = doc_images.shape[0]
    doc_ends = jnp.cumsum(doc_images)
    positions = jnp.arange(images, dtype=jnp.int32)
    doc_of = jnp.sum((positions[:, None] >= doc_ends[None, :]).astype(jnp.int32), axis=1)
    doc_index = jnp.arange(documents, dtype=jnp.int32)
    end_of = jnp.sum(jnp.where(doc_index[None, :] == doc_of[:, None], doc_ends[None, :], 0), axis=1)
    stop_at = jnp.sum(
        jnp.where(positions[None, :] == end_of[:, None], image_start[None, :], 0), axis=1
    )
    stop_at = stop_at + jnp.where(end_of >= images, total_spans, 0)
    return (span_ids[:, None] >= image_start[None, :]) & (span_ids[:, None] < stop_at[None, :])


NT = (((1,), (1,)), ((), ()))


def attention_kernel(bounds_ref, q_ref, k_ref, v_ref, t_ref, o_ref):
    first = bounds_ref[0]
    stop = bounds_ref[1]
    scaling = HD ** (-0.5)
    tokens, width = q_ref.shape
    heads = width // HD

    def stacked(ref):
        return jnp.concatenate([ref[:, h * HD : (h + 1) * HD] for h in range(heads)], axis=0)

    @pl.when(stop <= first)
    def _():
        o_ref[...] = jnp.zeros_like(o_ref)

    @pl.when(stop > first)
    def _():
        row = lax.broadcasted_iota(jnp.int32, (1, KEYS_PAD), 1)
        bias = jnp.where((row >= first) & (row < stop), 0.0, NEG)
        q = stacked(q_ref).astype(jnp.bfloat16)
        k = k_ref[...]
        v = v_ref[...]
        s = lax.dot_general(q, k, NT, preferred_element_type=jnp.float32) * scaling + bias
        peak = jnp.max(s, axis=-1, keepdims=True)
        w = jnp.exp(s - peak)
        total = jnp.sum(w, axis=-1, keepdims=True)
        acc = jnp.dot(w.astype(jnp.bfloat16), v, preferred_element_type=jnp.float32)
        inv = 1.0 / jnp.maximum(total, 1.0)
        attended = acc * inv
        out_grad = (1024.0 * (attended - stacked(t_ref).astype(jnp.float32))).astype(jnp.bfloat16)
        delta = jnp.sum(out_grad.astype(jnp.float32) * attended, axis=-1, keepdims=True)
        dp = lax.dot_general(out_grad, v, NT, preferred_element_type=jnp.float32)
        ds = (w * ((dp - delta) * (inv * scaling))).astype(jnp.bfloat16)
        g = jnp.dot(ds, k, preferred_element_type=jnp.float32).astype(o_ref.dtype)
        for h in range(heads):
            o_ref[:, h * HD : (h + 1) * HD] = g[h * tokens : (h + 1) * tokens]


def attention(bounds, queries, keys, values, target, chunk):
    tokens, width = queries.shape
    pair = 2 * HD
    steps = width // pair
    group = (H // KVH) * HD
    base = chunk * steps

    def kv_map(i, b):
        return (0, ((base + i) * pair) // group)

    return pl.pallas_call(
        attention_kernel,
        out_shape=jax.ShapeDtypeStruct((tokens, width), jnp.bfloat16),
        grid_spec=pltpu.PrefetchScalarGridSpec(
            num_scalar_prefetch=1,
            grid=(steps,),
            in_specs=[
                pl.BlockSpec((tokens, pair), lambda i, b: (0, i)),
                pl.BlockSpec((KEYS_PAD, HD), kv_map),
                pl.BlockSpec((KEYS_PAD, HD), kv_map),
                pl.BlockSpec((tokens, pair), lambda i, b: (0, base + i)),
            ],
            out_specs=pl.BlockSpec((tokens, pair), lambda i, b: (0, i)),
        ),
        compiler_params=pltpu.CompilerParams(vmem_limit_bytes=44 << 20),
        cost_estimate=pl.CostEstimate(
            flops=20 * tokens * width * KEYS_PAD // 2,
            bytes_accessed=4 * KEYS_PAD * HD + 8 * tokens * width,
            transcendentals=tokens * (width // HD) * KEYS_PAD,
        ),
        name="attention",
    )(bounds, queries, keys, values, target)


def final_kernel(x_ref, g_ref, r_ref, c_ref, *rest):
    o_ref = rest[-1]
    wg = jnp.dot(x_ref[...], g_ref[...], preferred_element_type=jnp.float32)
    t = jnp.tanh(0.5 * r_ref[...])
    t2 = t * t
    o_ref[...] = (wg * (0.3 * c_ref[...]) - (4.0 * 1.728 * 0.3) * (t2 * t)) * (1.0 - t2)


def final(spread_t, grad, logits, steps, previous, chunk):
    rows, tokens = spread_t.shape
    width = grad.shape[1]
    tm = 256
    in_specs = [
        pl.BlockSpec((tm, tokens), lambda i: (i, 0)),
        pl.BlockSpec((tokens, width), lambda i: (0, 0)),
        pl.BlockSpec((tm, width), lambda i: (i, chunk)),
        pl.BlockSpec((1, width), lambda i: (0, chunk)),
    ]
    args = [spread_t, grad, logits, steps]
    aliases = {}
    if previous is not None:
        in_specs.append(pl.BlockSpec(memory_space=pl.ANY))
        args.append(previous)
        aliases = {4: 0}
    return pl.pallas_call(
        final_kernel,
        out_shape=jax.ShapeDtypeStruct(logits.shape, jnp.float32),
        grid=(rows // tm,),
        in_specs=in_specs,
        out_specs=pl.BlockSpec((tm, width), lambda i: (i, chunk)),
        input_output_aliases=aliases,
        compiler_params=pltpu.CompilerParams(vmem_limit_bytes=40 << 20),
        cost_estimate=pl.CostEstimate(
            flops=2 * rows * tokens * width,
            bytes_accessed=8 * rows * width + 2 * tokens * (rows + width),
            transcendentals=rows * width,
        ),
        name="final",
    )(*args)


FIXED = 32767.0


def exchange_sum(part, tok_dev):
    n_text = lax.axis_size("text")
    me = lax.axis_index("text")
    width = part.shape[1]
    heads = width // HD

    def rows_of(owner):
        return lax.dynamic_slice_in_dim(part, owner * tok_dev, tok_dev, 0)

    total = rows_of(me).reshape(tok_dev, heads, HD)
    for shift in range(1, n_text):
        perm = [(i, (i + shift) % n_text) for i in range(n_text)]
        rows = rows_of((me + shift) % n_text).reshape(tok_dev, heads, HD)
        largest = jnp.maximum(jnp.max(jnp.abs(rows), axis=-1), 1e-30)
        levels = jnp.round(rows * (FIXED / largest)[..., None]).astype(jnp.int16)
        levels = lax.ppermute(levels.reshape(tok_dev, width), "text", perm)
        largest = lax.ppermute(largest.T, "text", perm).T
        levels = levels.reshape(tok_dev, heads, HD).astype(jnp.float32)
        total = total + levels * (largest * (1.0 / FIXED))[..., None]
    return total.reshape(tok_dev, width)


def per_device(
    text_states,
    grid_levels,
    round_logits,
    column_steps,
    image_keys,
    image_values,
    target_out,
    doc_images,
    image_start,
):
    tok_dev = text_states.shape[0]
    out_cols = grid_levels.shape[1]
    n_text = lax.axis_size("text")
    assert tok_dev == SPAN
    images = image_start.shape[0]
    steps_row = column_steps[None, :]

    n_image = lax.axis_size("image")
    share = text_states.shape[1] // (n_text * n_image)
    own = lax.dynamic_index_in_dim(
        text_states.reshape(tok_dev, n_text, n_image, share),
        lax.axis_index("image"),
        2,
        keepdims=False,
    )
    own = lax.all_to_all(own.transpose(1, 0, 2), "text", split_axis=0, concat_axis=0, tiled=True)
    shares = lax.all_gather(own.reshape(n_text * tok_dev, share), "image", axis=0)
    spread = shares.transpose(1, 0, 2).reshape(n_text * tok_dev, n_image * share)
    soft = 0.5 + 0.6 * jnp.tanh(0.5 * round_logits)
    weight_q = (steps_row * (grid_levels.astype(jnp.float32) + soft)).astype(jnp.bfloat16)
    weight_q = lax.optimization_barrier(weight_q)

    span_ids = jnp.reshape(lax.axis_index("text"), (1,)).astype(jnp.int32)
    visible = visibility(span_ids, doc_images, image_start, n_text)[0]
    seen_before = jnp.cumsum(visible.astype(jnp.int32))
    count = seen_before[-1]
    lowest = jnp.sum((seen_before == 0).astype(jnp.int32))
    base = jnp.minimum(lowest, images - MAX_SEEN)
    first = (lowest - base) * IMG_TOK
    bounds = jnp.stack([first, first + count * IMG_TOK]).astype(jnp.int32)

    def window(array):
        rows = lax.dynamic_slice_in_dim(array, base * IMG_TOK, KEYS, 0)
        return jnp.pad(rows, ((0, KEYS_PAD - KEYS), (0, 0)))

    keys = window(image_keys)
    values = window(image_values)

    width = out_cols // CHUNKS
    grads = []
    sums = []
    for c in range(CHUNKS):
        part = jnp.dot(
            spread, weight_q[:, c * width : (c + 1) * width], preferred_element_type=jnp.float32
        )
        sums.append(exchange_sum(part, tok_dev))
    for c in range(CHUNKS):
        local = attention(bounds, sums[c], keys, values, target_out, c)
        grads.append(lax.all_gather(local, "text", axis=0, tiled=True))
    spread_t = spread.T
    result = None
    for c in range(CHUNKS):
        result = final(spread_t, grads[c], round_logits, steps_row, result, c)
    return result


def solution(mesh):
    placed = (
        P(("groups", "text"), None),
        P(("groups", "text"), "image"),
        P(("groups", "text"), "image"),
        P(("groups", "image")),
        P("groups", "image"),
        P("groups", "image"),
        P(("groups", "text"), "image"),
        P("groups"),
        P("groups"),
    )
    return jax.shard_map(
        per_device,
        mesh=mesh,
        in_specs=placed,
        out_specs=P(("groups", "text"), "image"),
        check_vma=False,
    )
```

```python
import functools

import jax
import jax.numpy as jnp
from jax import lax
from jax.experimental import pallas as pl
from jax.experimental.pallas import tpu as pltpu
from jax.sharding import PartitionSpec as P

H = 64
KVH = 8
HD = 128
IMG_TOK = 1601
SPAN = 128
MAX_SEEN = 2
KEYS = MAX_SEEN * IMG_TOK
KEYS_PAD = -(-KEYS // 256) * 256
CHUNKS = 4
NEG = -1e30


def visibility(span_ids, doc_images, image_start, total_spans):
    images = image_start.shape[0]
    documents = doc_images.shape[0]
    doc_ends = jnp.cumsum(doc_images)
    positions = jnp.arange(images, dtype=jnp.int32)
    doc_of = jnp.sum((positions[:, None] >= doc_ends[None, :]).astype(jnp.int32), axis=1)
    doc_index = jnp.arange(documents, dtype=jnp.int32)
    end_of = jnp.sum(jnp.where(doc_index[None, :] == doc_of[:, None], doc_ends[None, :], 0), axis=1)
    stop_at = jnp.sum(
        jnp.where(positions[None, :] == end_of[:, None], image_start[None, :], 0), axis=1
    )
    stop_at = stop_at + jnp.where(end_of >= images, total_spans, 0)
    return (span_ids[:, None] >= image_start[None, :]) & (span_ids[:, None] < stop_at[None, :])


NT = (((1,), (1,)), ((), ()))


def attention_kernel(bounds_ref, q_ref, k_ref, v_ref, t_ref, o_ref):
    first = bounds_ref[0]
    stop = bounds_ref[1]
    scaling = HD ** (-0.5)
    tokens, width = q_ref.shape
    heads = width // HD

    def stacked(ref):
        return jnp.concatenate([ref[:, h * HD : (h + 1) * HD] for h in range(heads)], axis=0)

    @pl.when(stop <= first)
    def _():
        o_ref[...] = jnp.zeros_like(o_ref)

    @pl.when(stop > first)
    def _():
        row = lax.broadcasted_iota(jnp.int32, (1, KEYS_PAD), 1)
        bias = jnp.where((row >= first) & (row < stop), 0.0, NEG)
        q = stacked(q_ref).astype(jnp.bfloat16)
        k = k_ref[...]
        v = v_ref[...]
        s = lax.dot_general(q, k, NT, preferred_element_type=jnp.float32) * scaling + bias
        peak = jnp.max(s, axis=-1, keepdims=True)
        w = jnp.exp(s - peak)
        total = jnp.sum(w, axis=-1, keepdims=True)
        acc = jnp.dot(w.astype(jnp.bfloat16), v, preferred_element_type=jnp.float32)
        inv = 1.0 / jnp.maximum(total, 1.0)
        attended = acc * inv
        out_grad = (1024.0 * (attended - stacked(t_ref).astype(jnp.float32))).astype(jnp.bfloat16)
        delta = jnp.sum(out_grad.astype(jnp.float32) * attended, axis=-1, keepdims=True)
        dp = lax.dot_general(out_grad, v, NT, preferred_element_type=jnp.float32)
        ds = (w * ((dp - delta) * (inv * scaling))).astype(jnp.bfloat16)
        g = jnp.dot(ds, k, preferred_element_type=jnp.float32).astype(o_ref.dtype)
        for h in range(heads):
            o_ref[:, h * HD : (h + 1) * HD] = g[h * tokens : (h + 1) * tokens]


def attention(bounds, queries, keys, values, target, chunk):
    tokens, width = queries.shape
    pair = 2 * HD
    steps = width // pair
    group = (H // KVH) * HD
    base = chunk * steps

    def kv_map(i, b):
        return (0, ((base + i) * pair) // group)

    return pl.pallas_call(
        attention_kernel,
        out_shape=jax.ShapeDtypeStruct((tokens, width), jnp.bfloat16),
        grid_spec=pltpu.PrefetchScalarGridSpec(
            num_scalar_prefetch=1,
            grid=(steps,),
            in_specs=[
                pl.BlockSpec((tokens, pair), lambda i, b: (0, i)),
                pl.BlockSpec((KEYS_PAD, HD), kv_map),
                pl.BlockSpec((KEYS_PAD, HD), kv_map),
                pl.BlockSpec((tokens, pair), lambda i, b: (0, base + i)),
            ],
            out_specs=pl.BlockSpec((tokens, pair), lambda i, b: (0, i)),
        ),
        compiler_params=pltpu.CompilerParams(vmem_limit_bytes=44 << 20),
        cost_estimate=pl.CostEstimate(
            flops=20 * tokens * width * KEYS_PAD // 2,
            bytes_accessed=4 * KEYS_PAD * HD + 8 * tokens * width,
            transcendentals=tokens * (width // HD) * KEYS_PAD,
        ),
        name="attention",
    )(bounds, queries, keys, values, target)


def final_kernel(x_ref, g_ref, r_ref, c_ref, *rest):
    o_ref = rest[-1]
    wg = jnp.dot(x_ref[...], g_ref[...], preferred_element_type=jnp.float32)
    t = jnp.tanh(0.5 * r_ref[...])
    t2 = t * t
    o_ref[...] = (wg * (0.3 * c_ref[...]) - (4.0 * 1.728 * 0.3) * (t2 * t)) * (1.0 - t2)


def final(spread_t, grad, logits, steps, previous, chunk):
    rows, tokens = spread_t.shape
    width = grad.shape[1]
    tm = 256
    in_specs = [
        pl.BlockSpec((tm, tokens), lambda i: (i, 0)),
        pl.BlockSpec((tokens, width), lambda i: (0, 0)),
        pl.BlockSpec((tm, width), lambda i: (i, chunk)),
        pl.BlockSpec((1, width), lambda i: (0, chunk)),
    ]
    args = [spread_t, grad, logits, steps]
    aliases = {}
    if previous is not None:
        in_specs.append(pl.BlockSpec(memory_space=pl.ANY))
        args.append(previous)
        aliases = {4: 0}
    return pl.pallas_call(
        final_kernel,
        out_shape=jax.ShapeDtypeStruct(logits.shape, jnp.float32),
        grid=(rows // tm,),
        in_specs=in_specs,
        out_specs=pl.BlockSpec((tm, width), lambda i: (i, chunk)),
        input_output_aliases=aliases,
        compiler_params=pltpu.CompilerParams(vmem_limit_bytes=40 << 20),
        cost_estimate=pl.CostEstimate(
            flops=2 * rows * tokens * width,
            bytes_accessed=8 * rows * width + 2 * tokens * (rows + width),
            transcendentals=rows * width,
        ),
        name="final",
    )(*args)


def per_device(
    text_states,
    grid_levels,
    round_logits,
    column_steps,
    image_keys,
    image_values,
    target_out,
    doc_images,
    image_start,
):
    tok_dev = text_states.shape[0]
    out_cols = grid_levels.shape[1]
    n_text = lax.axis_size("text")
    assert tok_dev == SPAN
    images = image_start.shape[0]
    steps_row = column_steps[None, :]

    n_image = lax.axis_size("image")
    share = text_states.shape[1] // (n_text * n_image)
    own = lax.dynamic_index_in_dim(
        text_states.reshape(tok_dev, n_text, n_image, share),
        lax.axis_index("image"),
        2,
        keepdims=False,
    )
    own = lax.all_to_all(own.transpose(1, 0, 2), "text", split_axis=0, concat_axis=0, tiled=True)
    shares = lax.all_gather(own.reshape(n_text * tok_dev, share), "image", axis=0)
    spread = shares.transpose(1, 0, 2).reshape(n_text * tok_dev, n_image * share)
    soft = 0.5 + 0.6 * jnp.tanh(0.5 * round_logits)
    weight_q = (steps_row * (grid_levels.astype(jnp.float32) + soft)).astype(jnp.bfloat16)
    weight_q = lax.optimization_barrier(weight_q)

    span_ids = jnp.reshape(lax.axis_index("text"), (1,)).astype(jnp.int32)
    visible = visibility(span_ids, doc_images, image_start, n_text)[0]
    seen_before = jnp.cumsum(visible.astype(jnp.int32))
    count = seen_before[-1]
    lowest = jnp.sum((seen_before == 0).astype(jnp.int32))
    base = jnp.minimum(lowest, images - MAX_SEEN)
    first = (lowest - base) * IMG_TOK
    bounds = jnp.stack([first, first + count * IMG_TOK]).astype(jnp.int32)

    def window(array):
        rows = lax.dynamic_slice_in_dim(array, base * IMG_TOK, KEYS, 0)
        return jnp.pad(rows, ((0, KEYS_PAD - KEYS), (0, 0)))

    keys = window(image_keys)
    values = window(image_values)

    width = out_cols // CHUNKS
    grads = []
    sums = []
    for c in range(CHUNKS):
        part = jnp.dot(
            spread, weight_q[:, c * width : (c + 1) * width], preferred_element_type=jnp.float32
        )
        sums.append(lax.psum_scatter(part, "text", scatter_dimension=0, tiled=True))
    for c in range(CHUNKS):
        local = attention(bounds, sums[c], keys, values, target_out, c)
        grads.append(lax.all_gather(local, "text", axis=0, tiled=True))
    spread_t = spread.T
    result = None
    for c in range(CHUNKS):
        result = final(spread_t, grads[c], round_logits, steps_row, result, c)
    return result


def solution(mesh):
    placed = (
        P(("groups", "text"), None),
        P(("groups", "text"), "image"),
        P(("groups", "text"), "image"),
        P(("groups", "image")),
        P("groups", "image"),
        P("groups", "image"),
        P(("groups", "text"), "image"),
        P("groups"),
        P("groups"),
    )
    return jax.shard_map(
        per_device,
        mesh=mesh,
        in_specs=placed,
        out_specs=P(("groups", "text"), "image"),
        check_vma=False,
    )
```
